32 devices in a mesh: parts: 2 (over y), seq: 16 (over z, x, core).
Axes of the slice: x: 2, y: 2, z: 4, core: 2. Of those that a mesh axis runs over, the one named last changes fastest.
Arguments:
- queries: float32 [4096, 4096], P(('parts', 'seq')), parts along dimension 0, may hold values from -11 to 11
- visual_keys: float32 [4096, 512], P(('parts', 'seq')), parts along dimension 0, may hold values from -4 to 4
- visual_value_rows: float32 [4096, 512], P(('parts', 'seq')), parts along dimension 0, may hold values from -6 to 6
- output_gradient: float32 [4096, 4096], P(('parts', 'seq')), parts along dimension 0, may hold values from -6 to 6
- query_head_gate: float32 [32], replicated, may hold values from 0.3 to 2
- window_lists: int32 [2, 6], P('parts'), parts along dimension 0, may hold values from 0 to 15, as said below
- block_place: int32 [32], P('parts'), parts along dimension 0, may hold values from 0 to 15, each once
Outputs:
- output: float32 [4096, 4096], P(('parts', 'seq')), parts along dimension 0
- grad_queries: float32 [4096, 4096], P(('parts', 'seq')), parts along dimension 0
- grad_keys: float32 [4096, 512], P(('parts', 'seq')), parts along dimension 0
- grad_values: float32 [4096, 512], P(('parts', 'seq')), parts along dimension 0
The draws below stay inside these ranges and needn't reach their ends.
There are 2 independent parts, one for each index of `parts`. The reference program is written for one: setup_inputs(seed, part) draws one part's arguments, and reference() takes and returns one part's arrays. A program takes and returns all parts, laid end to end along the dimension named above; an argument that names none is the same for every part. Nothing has to cross between parts.
Inputs may be any that keep to these rules, and one draw needn't show every extreme that they name: `window_lists`: each row names 6 different visual blocks.
All inputs are finite; a program needn't handle non-finite values.
Results may differ from the reference program's by a relative error of at most 0.0003.
Values sent between devices are 32-bit elements; how exact they have to be, the bound alone decides.
A program may use at most 128 MiB of HBM per device.

```python
import jax
import jax.numpy as jnp
from jax import lax

QUERY_HEADS = 32
KEY_VALUE_HEADS = 4
HEAD_FEATURES = 128
BLOCK_TOKENS = 128
LISTED_BLOCKS = 6
WINDOW_ROWS = 2048
TEXT = 2048
WINDOWS = 1
VBLOCKS = 16
VISUAL_TOKENS = 2048


def draw_visual_keys(key, part):
    gaussian_draw = jax.random.normal(jax.random.fold_in(key, 3), (VISUAL_TOKENS, KEY_VALUE_HEADS * HEAD_FEATURES), jnp.float32)
    return jnp.clip(gaussian_draw, -4.0, 4.0)


def draw_queries(key, part):
    gaussian_draw = jax.random.normal(jax.random.fold_in(key, 6), (TEXT, QUERY_HEADS * HEAD_FEATURES), jnp.float32)
    return jnp.clip(gaussian_draw, -4.0, 4.0)


def draw_window_lists(key, part):
    raw_scores = jax.random.randint(jax.random.fold_in(key, 4711), (WINDOWS, VBLOCKS), 0, 1 << 20, jnp.int32)
    distinct_scores = raw_scores * VBLOCKS + jnp.arange(VBLOCKS, dtype=jnp.int32)[None, :]
    ranking = jnp.argsort(-distinct_scores, axis=1, stable=True)
    return ranking[:, :LISTED_BLOCKS].astype(jnp.int32)


def levels(own_key, shape, pieces, low, high):
    loudness = 1.0
    for axis_at, blocks in pieces:
        draws = jax.random.uniform(jax.random.fold_in(jax.random.fold_in(own_key, 6), axis_at), (blocks,), jnp.float32, low / len(pieces), high / len(pieces))
        loudness = loudness * jnp.repeat(jnp.exp(draws), shape[axis_at] // blocks).reshape((-1,) + (1,) * (len(shape) - 1 - axis_at))
    return loudness


def normal_values(own_key, extent, spread, most, shards=(), held_as=jnp.bfloat16):
    loudness = levels(own_key, extent, shards, -0.22, 0.18) if shards else 1.0
    values = jax.random.normal(own_key, extent, jnp.float32) * spread * loudness
    return jnp.minimum(jnp.maximum(values, -most), most).astype(held_as)


def setup_inputs(seed: int = 0, part: int = 0) -> dict:
    seeds = jax.random.split(jax.random.key(seed), 8)
    own_keys = jax.random.split(jax.random.fold_in(seeds[7], part), 8)
    queries = draw_queries(jax.random.fold_in(jax.random.fold_in(seeds[7], part), 71), part)
    visual_keys = draw_visual_keys(jax.random.fold_in(jax.random.fold_in(seeds[7], part), 71), part)
    visual_value_rows = normal_values(own_keys[2], (VISUAL_TOKENS, KEY_VALUE_HEADS * HEAD_FEATURES), 1.0, 6.0, ((0, 16),), jnp.float32)
    output_gradient = normal_values(own_keys[3], (TEXT, QUERY_HEADS * HEAD_FEATURES), 1.0, 6.0, ((0, 16),), jnp.float32)
    query_head_gate = jnp.clip(jax.random.uniform(seeds[4], (QUERY_HEADS,), jnp.float32, 0.3, 2.0), 0.3, 2.0)
    window_lists = draw_window_lists(jax.random.fold_in(jax.random.fold_in(seeds[7], part), 71), part)
    block_place = jax.random.permutation(own_keys[6], VBLOCKS).astype(jnp.int32)
    return dict(queries=queries, visual_keys=visual_keys, visual_value_rows=visual_value_rows, output_gradient=output_gradient, query_head_gate=query_head_gate, window_lists=window_lists, block_place=block_place)


HIGHEST = lax.Precision.HIGHEST


def attend(window_query_rows, window_key_rows, window_value_rows, gradient_rows, gate_lookup):
    inverse_root = HEAD_FEATURES ** -0.5
    scores = jnp.einsum('rkgd,skd->kgrs', window_query_rows, window_key_rows, precision=HIGHEST) * inverse_root
    row_max = jnp.max(scores, axis=-1, keepdims=True)
    raised = jnp.exp(scores - row_max)
    weights = raised / jnp.sum(raised, axis=-1, keepdims=True)
    attended = jnp.einsum('kgrs,skd->rkgd', weights, window_value_rows, precision=HIGHEST)
    output = attended * gate_lookup[None, :, :, None]
    grad_attended = gradient_rows * gate_lookup[None, :, :, None]
    row_dot = jnp.einsum('rkgd,rkgd->kgr', grad_attended, attended, precision=HIGHEST)
    grad_weights = jnp.einsum('rkgd,skd->kgrs', grad_attended, window_value_rows, precision=HIGHEST)
    grad_scores = weights * (grad_weights - row_dot[..., None])
    grad_query = jnp.einsum('kgrs,skd->rkgd', grad_scores, window_key_rows, precision=HIGHEST) * inverse_root
    grad_key = jnp.einsum('kgrs,rkgd->skd', grad_scores, window_query_rows, precision=HIGHEST) * inverse_root
    grad_value = jnp.einsum('kgrs,rkgd->skd', weights, grad_attended, precision=HIGHEST)
    return output, grad_query, grad_key, grad_value


def reference(queries, visual_keys, visual_value_rows, output_gradient, query_head_gate, window_lists, block_place):
    queries_per_group = QUERY_HEADS // KEY_VALUE_HEADS
    feature_width = KEY_VALUE_HEADS * HEAD_FEATURES
    gate_lookup = jnp.tanh(query_head_gate).reshape(KEY_VALUE_HEADS, queries_per_group)
    gathered_key_block = visual_keys.reshape(VBLOCKS, BLOCK_TOKENS, feature_width)
    gathered_value_block = visual_value_rows.reshape(VBLOCKS, BLOCK_TOKENS, feature_width)
    window_count = TEXT // WINDOW_ROWS

    def one_window(window_index):
        picked_blocks = block_place[window_lists[window_index]]
        window_key_rows = gathered_key_block[picked_blocks].reshape(LISTED_BLOCKS * BLOCK_TOKENS, KEY_VALUE_HEADS, HEAD_FEATURES)
        window_value_rows = gathered_value_block[picked_blocks].reshape(LISTED_BLOCKS * BLOCK_TOKENS, KEY_VALUE_HEADS, HEAD_FEATURES)
        block_start = (window_index * WINDOW_ROWS).astype(jnp.int32)
        window_query_rows = lax.dynamic_slice_in_dim(queries, block_start, WINDOW_ROWS, 0).reshape(WINDOW_ROWS, KEY_VALUE_HEADS, queries_per_group, HEAD_FEATURES)
        gradient_rows = lax.dynamic_slice_in_dim(output_gradient, block_start, WINDOW_ROWS, 0).reshape(WINDOW_ROWS, KEY_VALUE_HEADS, queries_per_group, HEAD_FEATURES)
        output, grad_query, grad_key, grad_value = attend(window_query_rows, window_key_rows, window_value_rows, gradient_rows, gate_lookup)
        return (output.reshape(WINDOW_ROWS, QUERY_HEADS * HEAD_FEATURES), grad_query.reshape(WINDOW_ROWS, QUERY_HEADS * HEAD_FEATURES),
                grad_key.reshape(LISTED_BLOCKS, BLOCK_TOKENS, feature_width), grad_value.reshape(LISTED_BLOCKS, BLOCK_TOKENS, feature_width))

    results = lax.map(one_window, jnp.arange(window_count, dtype=jnp.int32))
    output = results[0].reshape(TEXT, QUERY_HEADS * HEAD_FEATURES)
    grad_queries = results[1].reshape(TEXT, QUERY_HEADS * HEAD_FEATURES)
    chosen_all = block_place[window_lists].reshape(-1)
    grad_keys = jnp.zeros((VBLOCKS, BLOCK_TOKENS, feature_width), jnp.float32).at[chosen_all].add(
        results[2].reshape(-1, BLOCK_TOKENS, feature_width)).reshape(VISUAL_TOKENS, feature_width)
    grad_values = jnp.zeros((VBLOCKS, BLOCK_TOKENS, feature_width), jnp.float32).at[chosen_all].add(
        results[3].reshape(-1, BLOCK_TOKENS, feature_width)).reshape(VISUAL_TOKENS, feature_width)
    return output, grad_queries, grad_keys, grad_values
```

```python
import functools
import math

import jax
import jax.numpy as jnp
from jax import lax
from jax.experimental import pallas as pl
from jax.experimental.pallas import tpu as pltpu
from jax.sharding import PartitionSpec as P

HEAD_FEATURES = 128
BLOCK_TOKENS = 128
WINDOW_ROWS = 2048
HIGHEST = lax.Precision.HIGHEST
MESH = pl.DeviceIdType.MESH
D = HEAD_FEATURES
HEADS_PER_STEP = 4


def split(x):
    hi = x.astype(jnp.bfloat16)
    return hi, (x - hi.astype(jnp.float32)).astype(jnp.bfloat16)


def dot(a, b):
    return jnp.dot(a, b, preferred_element_type=jnp.float32)


def load_head(k, v, kcat, vcat, kt2, vt2):
    kh, kl = split(k)
    kcat[...] = jnp.concatenate([kh, kl, kh], axis=1)
    vh, vl = split(v)
    vcat[...] = jnp.concatenate([vh, vl, vh], axis=1)
    th, tl = split(k.T)
    kt2[...] = jnp.concatenate([th, tl], axis=0)
    th, tl = split(v.T)
    vt2[...] = jnp.concatenate([th, tl], axis=0)


def heads_down(x):
    return jnp.concatenate([x[:, i : i + D] for i in range(0, x.shape[1], D)], axis=0)


def heads_across(x, rows):
    return jnp.concatenate([x[:, i : i + rows].T for i in range(0, x.shape[1], rows)], axis=1)


def attend_step(q, g, gate, kcat, vcat, kt2, vt2):
    inverse_root = D ** (-0.5)
    rows = q.shape[0]
    qr = heads_down(q) * inverse_root
    qt = qr.T
    th, tl = split(qt * math.log2(math.e))
    scores = dot(kcat[...], jnp.concatenate([th, th, tl], axis=0))
    row_max = jnp.max(scores, axis=0, keepdims=True)
    raised = jnp.exp2(scores - row_max)
    total = jnp.sum(raised, axis=0, keepdims=True)
    inv = 1.0 / total
    eh, el = split(raised)
    o2 = dot(vt2[...], eh)
    att = (o2[:D] + o2[D:] + dot(vt2[:D], el)) * inv
    out = heads_across(att, rows) * gate
    gt = heads_down(g * gate).T
    row_dot = jnp.sum(gt * att, axis=0, keepdims=True) * inv
    gt = gt * inv
    th, tl = split(gt)
    gw = dot(vcat[...], jnp.concatenate([th, th, tl], axis=0))
    ds = raised * (gw - row_dot)
    dh, dl = split(ds)
    q2 = dot(kt2[...], dh)
    gq = (q2[:D] + q2[D:] + dot(kt2[:D], dl)) * inverse_root
    gq = heads_across(gq, rows)
    gh, gl = split(gt.T)
    v2 = dot(eh, jnp.concatenate([gh, gl], axis=1))
    gv = v2[:, :D] + v2[:, D:] + dot(el, gh)
    qh, ql = split(qr)
    k2 = dot(dh, jnp.concatenate([qh, ql], axis=1))
    gk = k2[:, :D] + k2[:, D:] + dot(dl, qh)
    return out, gq, gk, gv


def attend_kernel(q_ref, g_ref, gate_ref, k_ref, v_ref, out_ref, gq_ref, gk_ref, gv_ref, kcat, vcat, kt2, vt2):
    first = pl.program_id(1) == 0

    @pl.when(first)
    def _():
        load_head(k_ref[...], v_ref[...], kcat, vcat, kt2, vt2)

    out, gq, gk, gv = attend_step(q_ref[...], g_ref[...], gate_ref[...], kcat, vcat, kt2, vt2)
    out_ref[...] = out
    gq_ref[...] = gq

    @pl.when(first)
    def _():
        gk_ref[...] = gk
        gv_ref[...] = gv

    @pl.when(jnp.logical_not(first))
    def _():
        gk_ref[...] += gk
        gv_ref[...] += gv


def attend(q, g, gate_row, k, v):
    rows, width = q.shape
    keys, kv_width = k.shape
    key_heads = kv_width // D
    wide = HEADS_PER_STEP * D
    steps = width // key_heads // wide
    big = pl.BlockSpec((rows, wide), lambda h, s: (0, h * steps + s))
    gate = pl.BlockSpec((1, wide), lambda h, s: (0, h * steps + s))
    kv = pl.BlockSpec((keys, D), lambda h, s: (0, h))
    f32 = jnp.float32
    return pl.pallas_call(
        attend_kernel,
        grid=(key_heads, steps),
        in_specs=[big, big, gate, kv, kv],
        out_specs=[big, big, kv, kv],
        out_shape=[
            jax.ShapeDtypeStruct(q.shape, f32),
            jax.ShapeDtypeStruct(q.shape, f32),
            jax.ShapeDtypeStruct(k.shape, f32),
            jax.ShapeDtypeStruct(k.shape, f32),
        ],
        scratch_shapes=[
            pltpu.VMEM((keys, 3 * D), jnp.bfloat16),
            pltpu.VMEM((keys, 3 * D), jnp.bfloat16),
            pltpu.VMEM((2 * D, keys), jnp.bfloat16),
            pltpu.VMEM((2 * D, keys), jnp.bfloat16),
        ],
        compiler_params=pltpu.CompilerParams(
            dimension_semantics=("arbitrary", "arbitrary"), vmem_limit_bytes=60 * 1024 * 1024
        ),
    )(q, g, gate_row, k, v)


def gate_row_of(query_head_gate):
    return jnp.repeat(jnp.tanh(query_head_gate), D)[None, :]


def local(
    queries,
    visual_keys,
    visual_value_rows,
    output_gradient,
    query_head_gate,
    window_lists,
    block_place,
):
    row_count = queries.shape[0]
    feature_width = visual_keys.shape[1]
    list_len = window_lists.shape[1]
    devices = lax.axis_size("seq")
    window_devices = WINDOW_ROWS // row_count
    blocks_here = visual_keys.shape[0] // BLOCK_TOKENS
    piece_len = BLOCK_TOKENS // devices
    channels = 2 * feature_width
    positions = devices * blocks_here
    stacked = jnp.concatenate([visual_keys, visual_value_rows], axis=1)
    stacked = stacked.reshape(blocks_here, devices, piece_len, channels)
    spread = lax.all_to_all(stacked, "seq", split_axis=1, concat_axis=0, tiled=True).reshape(
        positions, piece_len, channels
    )
    target_window = jnp.arange(devices, dtype=jnp.int32) // window_devices
    wanted = jnp.take(block_place, jnp.take(window_lists, target_window, axis=0), axis=0)
    fetched = lax.all_to_all(spread[wanted], "seq", split_axis=0, concat_axis=2, tiled=True)
    fetched = fetched.reshape(list_len * BLOCK_TOKENS, channels)
    output, grad_query, grad_key, grad_value = attend(
        queries,
        output_gradient,
        gate_row_of(query_head_gate),
        fetched[:, :feature_width],
        fetched[:, feature_width:],
    )
    gradients = jnp.concatenate([grad_key, grad_value], axis=1)
    collected = lax.all_to_all(
        gradients.reshape(list_len, devices, piece_len, channels),
        "seq",
        split_axis=1,
        concat_axis=1,
        tiled=True,
    )
    onehot = (wanted.T.reshape(1, -1) == jnp.arange(positions, dtype=jnp.int32)[:, None]).astype(
        jnp.float32
    )
    summed = jnp.dot(
        onehot,
        collected.reshape(list_len * devices, piece_len * channels),
        precision=HIGHEST,
        preferred_element_type=jnp.float32,
    )
    returned = lax.all_to_all(
        summed.reshape(devices, blocks_here, piece_len, channels),
        "seq",
        split_axis=0,
        concat_axis=2,
        tiled=True,
    )
    returned = returned.reshape(blocks_here * BLOCK_TOKENS, channels)
    return (output, grad_query, returned[:, :feature_width], returned[:, feature_width:])


def solution(mesh):
    rows = P(("parts", "seq"), None)
    return jax.shard_map(
        local,
        mesh=mesh,
        in_specs=(rows, rows, rows, rows, P(), P("parts", None), P("parts")),
        out_specs=(rows, rows, rows, rows),
        check_vma=False,
    )
```

```python
import functools
import math

import jax
import jax.numpy as jnp
from jax import lax
from jax.experimental import pallas as pl
from jax.experimental.pallas import tpu as pltpu
from jax.sharding import PartitionSpec as P

HEAD_FEATURES = 128
BLOCK_TOKENS = 128
WINDOW_ROWS = 2048
HIGHEST = lax.Precision.HIGHEST
MESH = pl.DeviceIdType.MESH
D = HEAD_FEATURES
HEADS_PER_STEP = 4


def split(x):
    hi = x.astype(jnp.bfloat16)
    return hi, (x - hi.astype(jnp.float32)).astype(jnp.bfloat16)


def dot(a, b):
    return jnp.dot(a, b, preferred_element_type=jnp.float32)


def load_head(k, v, kcat, vcat, kt2, vt2):
    kh, kl = split(k)
    kcat[...] = jnp.concatenate([kh, kl, kh], axis=1)
    vh, vl = split(v)
    vcat[...] = jnp.concatenate([vh, vl, vh], axis=1)
    th, tl = split(k.T)
    kt2[...] = jnp.concatenate([th, tl], axis=0)
    th, tl = split(v.T)
    vt2[...] = jnp.concatenate([th, tl], axis=0)


def heads_down(x):
    return jnp.concatenate([x[:, i : i + D] for i in range(0, x.shape[1], D)], axis=0)


def heads_across(x, rows):
    return jnp.concatenate([x[:, i : i + rows].T for i in range(0, x.shape[1], rows)], axis=1)


def attend_step(q, g, gate, kcat, vcat, kt2, vt2):
    inverse_root = D ** (-0.5)
    rows = q.shape[0]
    qr = heads_down(q) * inverse_root
    qt = qr.T
    th, tl = split(qt * math.log2(math.e))
    scores = dot(kcat[...], jnp.concatenate([th, th, tl], axis=0))
    row_max = jnp.max(scores, axis=0, keepdims=True)
    raised = jnp.exp2(scores - row_max)
    total = jnp.sum(raised, axis=0, keepdims=True)
    inv = 1.0 / total
    eh, el = split(raised)
    o2 = dot(vt2[...], eh)
    att = (o2[:D] + o2[D:] + dot(vt2[:D], el)) * inv
    out = heads_across(att, rows) * gate
    gt = heads_down(g * gate).T
    row_dot = jnp.sum(gt * att, axis=0, keepdims=True) * inv
    gt = gt * inv
    th, tl = split(gt)
    gw = dot(vcat[...], jnp.concatenate([th, th, tl], axis=0))
    ds = raised * (gw - row_dot)
    dh, dl = split(ds)
    q2 = dot(kt2[...], dh)
    gq = (q2[:D] + q2[D:] + dot(kt2[:D], dl)) * inverse_root
    gq = heads_across(gq, rows)
    gh, gl = split(gt.T)
    v2 = dot(eh, jnp.concatenate([gh, gl], axis=1))
    gv = v2[:, :D] + v2[:, D:] + dot(el, gh)
    qh, ql = split(qr)
    k2 = dot(dh, jnp.concatenate([qh, ql], axis=1))
    gk = k2[:, :D] + k2[:, D:] + dot(dl, qh)
    return out, gq, gk, gv


def attend_kernel(q_ref, g_ref, gate_ref, k_ref, v_ref, out_ref, gq_ref, gk_ref, gv_ref, kcat, vcat, kt2, vt2):
    first = pl.program_id(1) == 0

    @pl.when(first)
    def _():
        load_head(k_ref[...], v_ref[...], kcat, vcat, kt2, vt2)

    out, gq, gk, gv = attend_step(q_ref[...], g_ref[...], gate_ref[...], kcat, vcat, kt2, vt2)
    out_ref[...] = out
    gq_ref[...] = gq

    @pl.when(first)
    def _():
        gk_ref[...] = gk
        gv_ref[...] = gv

    @pl.when(jnp.logical_not(first))
    def _():
        gk_ref[...] += gk
        gv_ref[...] += gv


def attend(q, g, gate_row, k, v):
    rows, width = q.shape
    keys, kv_width = k.shape
    key_heads = kv_width // D
    wide = HEADS_PER_STEP * D
    steps = width // key_heads // wide
    big = pl.BlockSpec((rows, wide), lambda h, s: (0, h * steps + s))
    gate = pl.BlockSpec((1, wide), lambda h, s: (0, h * steps + s))
    kv = pl.BlockSpec((keys, D), lambda h, s: (0, h))
    f32 = jnp.float32
    return pl.pallas_call(
        attend_kernel,
        grid=(key_heads, steps),
        in_specs=[big, big, gate, kv, kv],
        out_specs=[big, big, kv, kv],
        out_shape=[
            jax.ShapeDtypeStruct(q.shape, f32),
            jax.ShapeDtypeStruct(q.shape, f32),
            jax.ShapeDtypeStruct(k.shape, f32),
            jax.ShapeDtypeStruct(k.shape, f32),
        ],
        scratch_shapes=[
            pltpu.VMEM((keys, 3 * D), jnp.bfloat16),
            pltpu.VMEM((keys, 3 * D), jnp.bfloat16),
            pltpu.VMEM((2 * D, keys), jnp.bfloat16),
            pltpu.VMEM((2 * D, keys), jnp.bfloat16),
        ],
        compiler_params=pltpu.CompilerParams(
            dimension_semantics=("arbitrary", "arbitrary"), vmem_limit_bytes=60 * 1024 * 1024
        ),
    )(q, g, gate_row, k, v)


def gate_row_of(query_head_gate):
    return jnp.repeat(jnp.tanh(query_head_gate), D)[None, :]


def fused_kernel(
    devices,
    k_ref,
    v_ref,
    gate_ref,
    lists_ref,
    place_ref,
    q_hbm,
    g_hbm,
    out_hbm,
    gq_hbm,
    gk_ref,
    gv_ref,
    cut,
    spread0,
    spread1,
    spread2,
    spread3,
    gathered,
    grads,
    sum1,
    sum2,
    recv3,
    back_out,
    back_in,
    q_buf,
    g_buf,
    out_buf,
    gq_buf,
    kcat,
    vcat,
    kt2,
    vt2,
    in_sem,
    out_sem,
    spread_send,
    spread_recv,
    z_send,
    z_recv,
    x_send,
    x_recv,
    s_send,
    s_recv,
    r1_send,
    r1_recv,
    r2_send,
    r2_recv,
    r3_send,
    r3_recv,
    back_send,
    back_recv,
):
    spread = (spread0, spread1, spread2, spread3)
    me = lax.axis_index("seq")
    c = lax.rem(me, 2)
    x = lax.rem(me // 2, 2)
    z = me // 4
    nz = devices // 4
    heads = k_ref.shape[1] // D
    piece = k_ref.shape[0] // devices
    listed = lists_ref.shape[1]
    keys = listed * BLOCK_TOKENS
    rows, width = q_buf.shape
    wide = HEADS_PER_STEP * D
    steps = width // heads // wide
    others = range(1, devices)
    along_z = range(1, nz)

    def device_at(z, x, c):
        return {"seq": (z * 2 + x) * 2 + c}

    def remote(src, dst, send, recv, device):
        return pltpu.make_async_remote_copy(
            src_ref=src,
            dst_ref=dst,
            send_sem=send,
            recv_sem=recv,
            device_id=device,
            device_id_type=MESH,
        )

    sibling = device_at(z, x, 1 - c)
    across = device_at(z, 1 - x, c)

    def load_copies(h):
        part = pl.ds(h * steps * wide, steps * wide)
        return [
            pltpu.make_async_copy(q_hbm.at[:, part], q_buf.at[:, part], in_sem.at[0, h]),
            pltpu.make_async_copy(g_hbm.at[:, part], g_buf.at[:, part], in_sem.at[1, h]),
        ]

    def store_copies(t):
        part = pl.ds(pl.multiple_of(t * wide, wide), wide)
        return [
            pltpu.make_async_copy(out_buf.at[:, part], out_hbm.at[:, part], out_sem.at[0, t]),
            pltpu.make_async_copy(gq_buf.at[:, part], gq_hbm.at[:, part], out_sem.at[1, t]),
        ]

    def spread_copies(h):
        copies = []
        for o in others:
            target = lax.rem(me + o, devices)
            copies.append(
                remote(
                    cut.at[h, target],
                    spread[h].at[me],
                    spread_send.at[h, o - 1],
                    spread_recv.at[h, o - 1],
                    {"seq": target},
                )
            )
        return copies

    def z_copies(h):
        own = gathered.at[h, c, x, z]
        return [
            remote(
                own,
                own,
                z_send.at[h, o - 1],
                z_recv.at[h, o - 1],
                device_at(lax.rem(z + o, nz), x, c),
            )
            for o in along_z
        ]

    def x_copies(h):
        half = gathered.at[h, c, x]
        return [remote(half, half, x_send.at[h], x_recv.at[h], across)]

    def s1_copies(h):
        half = gathered.at[h, c, x]
        return [remote(half, half, s_send.at[h, 0], s_recv.at[h, 0], sibling)]

    def s2_copies(h):
        half = gathered.at[h, c, 1 - x]
        return [remote(half, half, s_send.at[h, 1], s_recv.at[h, 1], sibling)]

    def r1_copies(h):
        return [remote(grads.at[h, 1 - c], sum1.at[h], r1_send.at[h], r1_recv.at[h], sibling)]

    def r2_copies(h):
        return [remote(sum1.at[h, 1 - x], sum2.at[h], r2_send.at[h], r2_recv.at[h], across)]

    def r3_copies(h):
        copies = []
        for o in along_z:
            target = lax.rem(z + o, nz)
            copies.append(
                remote(
                    sum2.at[h, target],
                    recv3.at[h, o - 1],
                    r3_send.at[h, o - 1],
                    r3_recv.at[h, o - 1],
                    device_at(target, x, c),
                )
            )
        return copies

    def back_copies(h):
        copies = []
        for o in others:
            target = lax.rem(me + o, devices)
            copies.append(
                remote(
                    back_out.at[h, target],
                    back_in.at[h, me],
                    back_send.at[h, o - 1],
                    back_recv.at[h, o - 1],
                    {"seq": target},
                )
            )
        return copies

    def start(copies):
        for copy in copies:
            copy.start()

    def arrive(copies):
        for copy in copies:
            copy.wait_recv()

    def wanted():
        return [place_ref[0, lists_ref[0, j]] for j in range(listed)]

    def select_and_send(h):
        arrive(spread_copies(h))
        for j, place in enumerate(wanted()):
            gathered[h, c, x, z, j * piece : (j + 1) * piece, :] = spread[h][place]
        start(z_copies(h))

    def forward_x(h):
        arrive(z_copies(h))
        start(x_copies(h))
        start(s1_copies(h))

    def forward_s(h):
        arrive(x_copies(h))
        start(s2_copies(h))

    def arrived(h):
        arrive(s1_copies(h))
        arrive(s2_copies(h))

    def reduce1(h):
        start(r1_copies(h))

    def reduce2(h):
        arrive(r1_copies(h))
        sum1[h] = sum1[h] + grads[h, c]
        start(r2_copies(h))

    def reduce3(h):
        arrive(r2_copies(h))
        sum2[h] = sum2[h] + sum1[h, x]
        start(r3_copies(h))

    def give_back(h):
        arrive(r3_copies(h))
        total = sum2[h, z]
        for o in along_z:
            total = total + recv3[h, o - 1]
        places = wanted()
        for d in range(devices):
            held = jnp.zeros((piece, 2 * D), jnp.float32)
            for j in range(listed):
                row = total[j * piece : (j + 1) * piece]
                held = jnp.where(jnp.full(held.shape, places[j]) == d, row, held)
            back_out[h, d] = held
        back_in[h, me] = back_out[h, me]
        start(back_copies(h))

    for h in range(heads):
        start(load_copies(h))
    barrier = pltpu.get_barrier_semaphore()
    for o in others:
        pl.semaphore_signal(
            barrier,
            inc=1,
            device_id={"seq": lax.rem(me + o, devices)},
            device_id_type=MESH,
        )
    for h in range(heads):
        part = slice(h * D, (h + 1) * D)
        both = jnp.concatenate([k_ref[:, part], v_ref[:, part]], axis=1)
        cut[h] = both.reshape(devices, piece, 2 * D)
        spread[h][me] = cut[h, me]
    pl.semaphore_wait(barrier, devices - 1)

    actions = {t: [] for t in range(-1, heads * steps)}

    def at(t, call, h):
        actions[min(t, heads * steps - 1)].append((call, h))

    last = heads - 1
    start(spread_copies(0))
    start(spread_copies(1))
    select_and_send(0)
    start(spread_copies(2))
    forward_x(0)
    select_and_send(1)
    start(spread_copies(3))
    forward_s(0)
    forward_x(1)
    arrived(0)

    at(0, forward_s, 1)
    at(0, select_and_send, 2)
    at(1, arrived, 1)
    at(1, forward_x, 2)
    at(1, select_and_send, 3)
    at(2, forward_s, 2)
    at(2, forward_x, 3)
    at(3, arrived, 2)
    at(3, forward_s, 3)
    at(5, arrived, 3)
    for h in range(heads):
        end = (h + 1) * steps - 1
        if h > 0:
            at(end, reduce3, h - 1)
        at(end, reduce1, h)
        if h > 0:
            at(end + 1, give_back, h - 1)
        at(end + 1, reduce2, h)
    at(heads * steps, reduce3, last)
    at(heads * steps, give_back, last)

    def step(t, carry):
        h = t // steps
        s = lax.rem(t, steps)

        @pl.when(s == 0)
        def _():
            both = gathered[h].reshape(keys, 2 * D)
            load_head(both[:, :D], both[:, D:], kcat, vcat, kt2, vt2)
            for copy in load_copies(h):
                copy.wait()

        part = pl.ds(pl.multiple_of(t * wide, wide), wide)
        gate = jnp.concatenate(
            [
                jnp.tanh(jnp.full((1, D), gate_ref[0, t * HEADS_PER_STEP + i], jnp.float32))
                for i in range(HEADS_PER_STEP)
            ],
            axis=1,
        )
        out, gq, gk, gv = attend_step(
            q_buf[:, part], g_buf[:, part], gate, kcat, vcat, kt2, vt2
        )
        out_buf[:, part] = out
        gq_buf[:, part] = gq
        start(store_copies(t))
        both = jnp.concatenate([gk, gv], axis=1).reshape(2, 2, nz, listed * piece, 2 * D)

        @pl.when(s == 0)
        def _():
            grads[h] = both

        @pl.when(s != 0)
        def _():
            grads[h] = grads[h] + both

        for when, calls in actions.items():
            if calls:

                @pl.when(t == when)
                def _(calls=calls):
                    for call, head in calls:
                        call(head)

        return carry

    lax.fori_loop(0, heads * steps, step, 0)

    for h in range(heads):
        arrive(back_copies(h))
        part = slice(h * D, (h + 1) * D)
        both = back_in[h].reshape(devices * piece, 2 * D)
        gk_ref[:, part] = both[:, :D]
        gv_ref[:, part] = both[:, D:]
    for h in range(heads):
        for make in (
            spread_copies,
            z_copies,
            x_copies,
            s1_copies,
            s2_copies,
            r1_copies,
            r2_copies,
            r3_copies,
            back_copies,
        ):
            for copy in make(h):
                copy.wait_send()
    for t in range(heads * steps):
        for copy in store_copies(t):
            copy.wait()


def fused(q, g, k, v, gate, lists, place):
    devices = lax.axis_size("seq")
    rows, width = q.shape
    heads = k.shape[1] // D
    listed = lists.shape[1]
    piece = k.shape[0] // devices
    nz = devices // 4
    keys = listed * BLOCK_TOKENS
    total_steps = width // (HEADS_PER_STEP * D)
    f32 = jnp.float32
    dma = pltpu.SemaphoreType.DMA
    vmem = pl.BlockSpec(memory_space=pltpu.VMEM)
    smem = pl.BlockSpec(memory_space=pltpu.SMEM)
    hbm = pl.BlockSpec(memory_space=pl.ANY)
    spread_shape = (heads, devices, piece, 2 * D)
    per_piece = (listed * piece, 2 * D)
    return pl.pallas_call(
        functools.partial(fused_kernel, devices),
        in_specs=[vmem, vmem, smem, smem, smem, hbm, hbm],
        out_specs=[hbm, hbm, vmem, vmem],
        out_shape=[
            jax.ShapeDtypeStruct(q.shape, f32),
            jax.ShapeDtypeStruct(q.shape, f32),
            jax.ShapeDtypeStruct(k.shape, f32),
            jax.ShapeDtypeStruct(k.shape, f32),
        ],
        scratch_shapes=[
            pltpu.VMEM(spread_shape, f32),
            pltpu.VMEM(spread_shape[1:], f32),
            pltpu.VMEM(spread_shape[1:], f32),
            pltpu.VMEM(spread_shape[1:], f32),
            pltpu.VMEM(spread_shape[1:], f32),
            pltpu.VMEM((heads, 2, 2, nz) + per_piece, f32),
            pltpu.VMEM((heads, 2, 2, nz) + per_piece, f32),
            pltpu.VMEM((heads, 2, nz) + per_piece, f32),
            pltpu.VMEM((heads, nz) + per_piece, f32),
            pltpu.VMEM((heads, nz - 1) + per_piece, f32),
            pltpu.VMEM(spread_shape, f32),
            pltpu.VMEM(spread_shape, f32),
            pltpu.VMEM((rows, width), f32),
            pltpu.VMEM((rows, width), f32),
            pltpu.VMEM((rows, width), f32),
            pltpu.VMEM((rows, width), f32),
            pltpu.VMEM((keys, 3 * D), jnp.bfloat16),
            pltpu.VMEM((keys, 3 * D), jnp.bfloat16),
            pltpu.VMEM((2 * D, keys), jnp.bfloat16),
            pltpu.VMEM((2 * D, keys), jnp.bfloat16),
            dma((2, heads)),
            dma((2, total_steps)),
            dma((heads, devices - 1)),
            dma((heads, devices - 1)),
            dma((heads, nz - 1)),
            dma((heads, nz - 1)),
            dma((heads,)),
            dma((heads,)),
            dma((heads, 2)),
            dma((heads, 2)),
            dma((heads,)),
            dma((heads,)),
            dma((heads,)),
            dma((heads,)),
            dma((heads, nz - 1)),
            dma((heads, nz - 1)),
            dma((heads, devices - 1)),
            dma((heads, devices - 1)),
        ],
        compiler_params=pltpu.CompilerParams(
            collective_id=0, has_side_effects=True, vmem_limit_bytes=60 * 1024 * 1024
        ),
    )(k, v, gate[None, :], lists, place[None, :], q, g)


def local(
    queries,
    visual_keys,
    visual_value_rows,
    output_gradient,
    query_head_gate,
    window_lists,
    block_place,
):
    row_count = queries.shape[0]
    feature_width = visual_keys.shape[1]
    list_len = window_lists.shape[1]
    devices = lax.axis_size("seq")
    window_devices = WINDOW_ROWS // row_count
    blocks_here = visual_keys.shape[0] // BLOCK_TOKENS
    piece_len = BLOCK_TOKENS // devices
    channels = 2 * feature_width
    positions = devices * blocks_here
    one_window = window_lists.shape[0] == 1 and devices == window_devices and blocks_here == 1
    if one_window and devices % 4 == 0 and devices > 4 and feature_width == 4 * D:
        return fused(
            queries,
            output_gradient,
            visual_keys,
            visual_value_rows,
            query_head_gate,
            window_lists,
            block_place,
        )
    stacked = jnp.concatenate([visual_keys, visual_value_rows], axis=1)
    stacked = stacked.reshape(blocks_here, devices, piece_len, channels)
    spread = lax.all_to_all(stacked, "seq", split_axis=1, concat_axis=0, tiled=True).reshape(
        positions, piece_len, channels
    )
    target_window = jnp.arange(devices, dtype=jnp.int32) // window_devices
    wanted = jnp.take(block_place, jnp.take(window_lists, target_window, axis=0), axis=0)
    fetched = lax.all_to_all(spread[wanted], "seq", split_axis=0, concat_axis=2, tiled=True)
    fetched = fetched.reshape(list_len * BLOCK_TOKENS, channels)
    output, grad_query, grad_key, grad_value = attend(
        queries,
        output_gradient,
        gate_row_of(query_head_gate),
        fetched[:, :feature_width],
        fetched[:, feature_width:],
    )
    gradients = jnp.concatenate([grad_key, grad_value], axis=1)
    collected = lax.all_to_all(
        gradients.reshape(list_len, devices, piece_len, channels),
        "seq",
        split_axis=1,
        concat_axis=1,
        tiled=True,
    )
    onehot = (wanted.T.reshape(1, -1) == jnp.arange(positions, dtype=jnp.int32)[:, None]).astype(
        jnp.float32
    )
    summed = jnp.dot(
        onehot,
        collected.reshape(list_len * devices, piece_len * channels),
        precision=HIGHEST,
        preferred_element_type=jnp.float32,
    )
    returned = lax.all_to_all(
        summed.reshape(devices, blocks_here, piece_len, channels),
        "seq",
        split_axis=0,
        concat_axis=2,
        tiled=True,
    )
    returned = returned.reshape(blocks_here * BLOCK_TOKENS, channels)
    return (output, grad_query, returned[:, :feature_width], returned[:, feature_width:])


def solution(mesh):
    rows = P(("parts", "seq"), None)
    return jax.shard_map(
        local,
        mesh=mesh,
        in_specs=(rows, rows, rows, rows, P(), P("parts", None), P("parts")),
        out_specs=(rows, rows, rows, rows),
        check_vma=False,
    )
```

```python
import functools
import math

import jax
import jax.numpy as jnp
from jax import lax
from jax.experimental import pallas as pl
from jax.experimental.pallas import tpu as pltpu
from jax.sharding import PartitionSpec as P

HEAD_FEATURES = 128
BLOCK_TOKENS = 128
WINDOW_ROWS = 2048
HIGHEST = lax.Precision.HIGHEST
MESH = pl.DeviceIdType.MESH
D = HEAD_FEATURES
HEADS_PER_STEP = 4


def split(x):
    hi = x.astype(jnp.bfloat16)
    return hi, (x - hi.astype(jnp.float32)).astype(jnp.bfloat16)


def dot(a, b):
    return jnp.dot(a, b, preferred_element_type=jnp.float32)


def load_head(k, v, kcat, vcat, kt2, vt2):
    kh, kl = split(k)
    kcat[...] = jnp.concatenate([kh, kl, kh], axis=1)
    vh, vl = split(v)
    vcat[...] = jnp.concatenate([vh, vl, vh], axis=1)
    th, tl = split(k.T)
    kt2[...] = jnp.concatenate([th, tl], axis=0)
    th, tl = split(v.T)
    vt2[...] = jnp.concatenate([th, tl], axis=0)


def heads_down(x):
    return jnp.concatenate([x[:, i : i + D] for i in range(0, x.shape[1], D)], axis=0)


def heads_across(x, rows):
    return jnp.concatenate([x[:, i : i + rows].T for i in range(0, x.shape[1], rows)], axis=1)


def attend_step(q, g, gate, kcat, vcat, kt2, vt2):
    inverse_root = D ** (-0.5)
    rows = q.shape[0]
    qr = heads_down(q) * inverse_root
    qt = qr.T
    th, tl = split(qt * math.log2(math.e))
    scores = dot(kcat[...], jnp.concatenate([th, th, tl], axis=0))
    row_max = jnp.max(scores, axis=0, keepdims=True)
    raised = jnp.exp2(scores - row_max)
    total = jnp.sum(raised, axis=0, keepdims=True)
    inv = 1.0 / total
    eh, el = split(raised)
    o2 = dot(vt2[...], eh)
    att = (o2[:D] + o2[D:] + dot(vt2[:D], el)) * inv
    out = heads_across(att, rows) * gate
    gt = heads_down(g * gate).T
    row_dot = jnp.sum(gt * att, axis=0, keepdims=True) * inv
    gt = gt * inv
    th, tl = split(gt)
    gw = dot(vcat[...], jnp.concatenate([th, th, tl], axis=0))
    ds = raised * (gw - row_dot)
    dh, dl = split(ds)
    q2 = dot(kt2[...], dh)
    gq = (q2[:D] + q2[D:] + dot(kt2[:D], dl)) * inverse_root
    gq = heads_across(gq, rows)
    gh, gl = split(gt.T)
    v2 = dot(eh, jnp.concatenate([gh, gl], axis=1))
    gv = v2[:, :D] + v2[:, D:] + dot(el, gh)
    qh, ql = split(qr)
    k2 = dot(dh, jnp.concatenate([qh, ql], axis=1))
    gk = k2[:, :D] + k2[:, D:] + dot(dl, qh)
    return out, gq, gk, gv


def attend_kernel(q_ref, g_ref, gate_ref, k_ref, v_ref, out_ref, gq_ref, gk_ref, gv_ref, kcat, vcat, kt2, vt2):
    first = pl.program_id(1) == 0

    @pl.when(first)
    def _():
        load_head(k_ref[...], v_ref[...], kcat, vcat, kt2, vt2)

    out, gq, gk, gv = attend_step(q_ref[...], g_ref[...], gate_ref[...], kcat, vcat, kt2, vt2)
    out_ref[...] = out
    gq_ref[...] = gq

    @pl.when(first)
    def _():
        gk_ref[...] = gk
        gv_ref[...] = gv

    @pl.when(jnp.logical_not(first))
    def _():
        gk_ref[...] += gk
        gv_ref[...] += gv


def attend(q, g, gate_row, k, v):
    rows, width = q.shape
    keys, kv_width = k.shape
    key_heads = kv_width // D
    wide = HEADS_PER_STEP * D
    steps = width // key_heads // wide
    big = pl.BlockSpec((rows, wide), lambda h, s: (0, h * steps + s))
    gate = pl.BlockSpec((1, wide), lambda h, s: (0, h * steps + s))
    kv = pl.BlockSpec((keys, D), lambda h, s: (0, h))
    f32 = jnp.float32
    return pl.pallas_call(
        attend_kernel,
        grid=(key_heads, steps),
        in_specs=[big, big, gate, kv, kv],
        out_specs=[big, big, kv, kv],
        out_shape=[
            jax.ShapeDtypeStruct(q.shape, f32),
            jax.ShapeDtypeStruct(q.shape, f32),
            jax.ShapeDtypeStruct(k.shape, f32),
            jax.ShapeDtypeStruct(k.shape, f32),
        ],
        scratch_shapes=[
            pltpu.VMEM((keys, 3 * D), jnp.bfloat16),
            pltpu.VMEM((keys, 3 * D), jnp.bfloat16),
            pltpu.VMEM((2 * D, keys), jnp.bfloat16),
            pltpu.VMEM((2 * D, keys), jnp.bfloat16),
        ],
        compiler_params=pltpu.CompilerParams(
            dimension_semantics=("arbitrary", "arbitrary"), vmem_limit_bytes=60 * 1024 * 1024
        ),
    )(q, g, gate_row, k, v)


def gate_row_of(query_head_gate):
    return jnp.repeat(jnp.tanh(query_head_gate), D)[None, :]


def fused_kernel(
    devices,
    k_ref,
    v_ref,
    gate_ref,
    lists_ref,
    place_ref,
    q_hbm,
    g_hbm,
    out_hbm,
    gq_hbm,
    gk_ref,
    gv_ref,
    cut,
    spread0,
    spread1,
    spread2,
    spread3,
    gathered,
    grads,
    sum1,
    sum2,
    recv3,
    back_out,
    back_in,
    q_buf,
    g_buf,
    out_buf,
    gq_buf,
    kcat,
    vcat,
    kt2,
    vt2,
    in_sem,
    out_sem,
    spread_send,
    spread_recv,
    z_send,
    z_recv,
    x_send,
    x_recv,
    s_send,
    s_recv,
    r1_send,
    r1_recv,
    r2_send,
    r2_recv,
    r3_send,
    r3_recv,
    back_send,
    back_recv,
):
    spread = (spread0, spread1, spread2, spread3)
    me = lax.axis_index("seq")
    c = lax.rem(me, 2)
    x = lax.rem(me // 2, 2)
    z = me // 4
    nz = devices // 4
    heads = k_ref.shape[1] // D
    piece = k_ref.shape[0] // devices
    listed = lists_ref.shape[1]
    keys = listed * BLOCK_TOKENS
    rows, width = q_buf.shape
    wide = HEADS_PER_STEP * D
    steps = width // heads // wide
    others = range(1, devices)
    along_z = range(1, nz)

    def device_at(z, x, c):
        return {"seq": (z * 2 + x) * 2 + c}

    def remote(src, dst, send, recv, device):
        return pltpu.make_async_remote_copy(
            src_ref=src,
            dst_ref=dst,
            send_sem=send,
            recv_sem=recv,
            device_id=device,
            device_id_type=MESH,
        )

    sibling = device_at(z, x, 1 - c)
    across = device_at(z, 1 - x, c)

    def load_copies(h):
        part = pl.ds(h * steps * wide, steps * wide)
        return [
            pltpu.make_async_copy(q_hbm.at[:, part], q_buf.at[:, part], in_sem.at[0, h]),
            pltpu.make_async_copy(g_hbm.at[:, part], g_buf.at[:, part], in_sem.at[1, h]),
        ]

    def store_copies(t):
        part = pl.ds(pl.multiple_of(t * wide, wide), wide)
        return [
            pltpu.make_async_copy(out_buf.at[:, part], out_hbm.at[:, part], out_sem.at[0, t]),
            pltpu.make_async_copy(gq_buf.at[:, part], gq_hbm.at[:, part], out_sem.at[1, t]),
        ]

    def spread_copies(h):
        copies = []
        for o in others:
            target = lax.rem(me + o, devices)
            copies.append(
                remote(
                    cut.at[h, target],
                    spread[h].at[me],
                    spread_send.at[h, o - 1],
                    spread_recv.at[h, o - 1],
                    {"seq": target},
                )
            )
        return copies

    def z_copies(h):
        own = gathered.at[h, c, x, z]
        return [
            remote(
                own,
                own,
                z_send.at[h, o - 1],
                z_recv.at[h, o - 1],
                device_at(lax.rem(z + o, nz), x, c),
            )
            for o in along_z
        ]

    def x_copies(h):
        copies = []
        for o in range(nz):
            own = gathered.at[h, c, x, lax.rem(z + nz - o, nz)]
            copies.append(remote(own, own, x_send.at[h, o], x_recv.at[h, o], across))
        return copies

    def s1_copies(h):
        half = gathered.at[h, c, x]
        return [remote(half, half, s_send.at[h, 0], s_recv.at[h, 0], sibling)]

    def s2_copies(h):
        half = gathered.at[h, c, 1 - x]
        return [remote(half, half, s_send.at[h, 1], s_recv.at[h, 1], sibling)]

    def r1_copies(h):
        return [remote(grads.at[h, 1 - c], sum1.at[h], r1_send.at[h], r1_recv.at[h], sibling)]

    def r2_copies(h):
        copies = []
        for o in range(nz):
            row = lax.rem(z + o, nz)
            copies.append(
                remote(
                    sum1.at[h, 1 - x, row],
                    sum2.at[h, row],
                    r2_send.at[h, o],
                    r2_recv.at[h, o],
                    across,
                )
            )
        return copies

    def r3_copies(h):
        copies = []
        for o in along_z:
            target = lax.rem(z + o, nz)
            copies.append(
                remote(
                    sum2.at[h, target],
                    recv3.at[h, o - 1],
                    r3_send.at[h, o - 1],
                    r3_recv.at[h, o - 1],
                    device_at(target, x, c),
                )
            )
        return copies

    def back_copies(h):
        copies = []
        for o in others:
            target = lax.rem(me + o, devices)
            copies.append(
                remote(
                    back_out.at[h, target],
                    back_in.at[h, me],
                    back_send.at[h, o - 1],
                    back_recv.at[h, o - 1],
                    {"seq": target},
                )
            )
        return copies

    def start(copies):
        for copy in copies:
            copy.start()

    def arrive(copies):
        for copy in copies:
            copy.wait_recv()

    def wanted():
        return [place_ref[0, lists_ref[0, j]] for j in range(listed)]

    def select_and_send(h):
        arrive(spread_copies(h))
        for j, place in enumerate(wanted()):
            gathered[h, c, x, z, j * piece : (j + 1) * piece, :] = spread[h][place]
        start(z_copies(h))
        start(x_copies(h)[:1])

    def forward_x(h):
        for o in along_z:
            arrive(z_copies(h)[o - 1 : o])
            start(x_copies(h)[o : o + 1])
        start(s1_copies(h))

    def forward_s(h):
        arrive(x_copies(h))
        start(s2_copies(h))

    def arrived(h):
        arrive(s1_copies(h))
        arrive(s2_copies(h))

    def reduce1(h):
        start(r1_copies(h))

    def reduce2(h):
        arrive(r1_copies(h))
        sum1[h] = sum1[h] + grads[h, c]
        copies = r2_copies(h)
        start(copies[1:] + copies[:1])

    def reduce3(h):
        for o in [*along_z, 0]:
            row = lax.rem(z + o, nz)
            arrive(r2_copies(h)[o : o + 1])
            sum2[h, row] = sum2[h, row] + sum1[h, x, row]
            if o:
                start(r3_copies(h)[o - 1 : o])

    def give_back(h):
        arrive(r3_copies(h))
        total = sum2[h, z]
        for o in along_z:
            total = total + recv3[h, o - 1]
        places = wanted()
        for d in range(devices):
            held = jnp.zeros((piece, 2 * D), jnp.float32)
            for j in range(listed):
                row = total[j * piece : (j + 1) * piece]
                held = jnp.where(jnp.full(held.shape, places[j]) == d, row, held)
            back_out[h, d] = held
        back_in[h, me] = back_out[h, me]
        start(back_copies(h))

    for h in range(heads):
        start(load_copies(h))
    barrier = pltpu.get_barrier_semaphore()
    for o in others:
        pl.semaphore_signal(
            barrier,
            inc=1,
            device_id={"seq": lax.rem(me + o, devices)},
            device_id_type=MESH,
        )
    for h in range(heads):
        part = slice(h * D, (h + 1) * D)
        both = jnp.concatenate([k_ref[:, part], v_ref[:, part]], axis=1)
        cut[h] = both.reshape(devices, piece, 2 * D)
        spread[h][me] = cut[h, me]
    pl.semaphore_wait(barrier, devices - 1)

    actions = {t: [] for t in range(-1, heads * steps)}

    def at(t, call, h):
        actions[min(t, heads * steps - 1)].append((call, h))

    last = heads - 1
    start(spread_copies(0))
    start(spread_copies(1))
    select_and_send(0)
    start(spread_copies(2))
    select_and_send(1)
    start(spread_copies(3))
    forward_x(0)
    select_and_send(2)
    forward_s(0)
    forward_x(1)
    arrived(0)

    at(0, select_and_send, 3)
    at(0, forward_s, 1)
    at(1, reduce1, 0)
    at(1, forward_x, 2)
    at(1, arrived, 1)
    at(2, forward_x, 3)
    at(2, forward_s, 2)
    at(2, reduce2, 0)
    at(3, reduce1, 1)
    at(3, arrived, 2)
    at(4, forward_s, 3)
    at(4, reduce2, 1)
    at(4, reduce3, 0)
    at(5, reduce1, 2)
    at(5, arrived, 3)
    at(5, give_back, 0)
    at(6, reduce2, 2)
    at(6, reduce3, 1)
    at(7, reduce1, last)
    at(7, give_back, 1)
    at(7, reduce2, last)
    at(7, reduce3, 2)
    at(7, reduce3, last)
    at(7, give_back, 2)
    at(7, give_back, last)

    def step(t, carry):
        h = t // steps
        s = lax.rem(t, steps)

        @pl.when(s == 0)
        def _():
            both = gathered[h].reshape(keys, 2 * D)
            load_head(both[:, :D], both[:, D:], kcat, vcat, kt2, vt2)
            for copy in load_copies(h):
                copy.wait()

        part = pl.ds(pl.multiple_of(t * wide, wide), wide)
        gate = jnp.concatenate(
            [
                jnp.tanh(jnp.full((1, D), gate_ref[0, t * HEADS_PER_STEP + i], jnp.float32))
                for i in range(HEADS_PER_STEP)
            ],
            axis=1,
        )
        out, gq, gk, gv = attend_step(
            q_buf[:, part], g_buf[:, part], gate, kcat, vcat, kt2, vt2
        )
        out_buf[:, part] = out
        gq_buf[:, part] = gq
        start(store_copies(t))
        both = jnp.concatenate([gk, gv], axis=1).reshape(2, 2, nz, listed * piece, 2 * D)

        @pl.when(s == 0)
        def _():
            grads[h] = both

        @pl.when(s != 0)
        def _():
            grads[h] = grads[h] + both

        for when, calls in actions.items():
            if calls:

                @pl.when(t == when)
                def _(calls=calls):
                    for call, head in calls:
                        call(head)

        return carry

    lax.fori_loop(0, heads * steps, step, 0)

    for h in range(heads):
        arrive(back_copies(h))
        part = slice(h * D, (h + 1) * D)
        both = back_in[h].reshape(devices * piece, 2 * D)
        gk_ref[:, part] = both[:, :D]
        gv_ref[:, part] = both[:, D:]
    for h in range(heads):
        for make in (
            spread_copies,
            z_copies,
            x_copies,
            s1_copies,
            s2_copies,
            r1_copies,
            r2_copies,
            r3_copies,
            back_copies,
        ):
            for copy in make(h):
                copy.wait_send()
    for t in range(heads * steps):
        for copy in store_copies(t):
            copy.wait()


def fused(q, g, k, v, gate, lists, place):
    devices = lax.axis_size("seq")
    rows, width = q.shape
    heads = k.shape[1] // D
    listed = lists.shape[1]
    piece = k.shape[0] // devices
    nz = devices // 4
    keys = listed * BLOCK_TOKENS
    total_steps = width // (HEADS_PER_STEP * D)
    f32 = jnp.float32
    dma = pltpu.SemaphoreType.DMA
    vmem = pl.BlockSpec(memory_space=pltpu.VMEM)
    smem = pl.BlockSpec(memory_space=pltpu.SMEM)
    hbm = pl.BlockSpec(memory_space=pl.ANY)
    far = pl.BlockSpec(memory_space=pltpu.HBM)
    spread_shape = (heads, devices, piece, 2 * D)
    per_piece = (listed * piece, 2 * D)
    return pl.pallas_call(
        functools.partial(fused_kernel, devices),
        in_specs=[vmem, vmem, smem, smem, smem, far, far],
        out_specs=[hbm, hbm, vmem, vmem],
        out_shape=[
            jax.ShapeDtypeStruct(q.shape, f32),
            jax.ShapeDtypeStruct(q.shape, f32),
            jax.ShapeDtypeStruct(k.shape, f32),
            jax.ShapeDtypeStruct(k.shape, f32),
        ],
        scratch_shapes=[
            pltpu.VMEM(spread_shape, f32),
            pltpu.VMEM(spread_shape[1:], f32),
            pltpu.VMEM(spread_shape[1:], f32),
            pltpu.VMEM(spread_shape[1:], f32),
            pltpu.VMEM(spread_shape[1:], f32),
            pltpu.VMEM((heads, 2, 2, nz) + per_piece, f32),
            pltpu.VMEM((heads, 2, 2, nz) + per_piece, f32),
            pltpu.VMEM((heads, 2, nz) + per_piece, f32),
            pltpu.VMEM((heads, nz) + per_piece, f32),
            pltpu.VMEM((heads, nz - 1) + per_piece, f32),
            pltpu.VMEM(spread_shape, f32),
            pltpu.VMEM(spread_shape, f32),
            pltpu.VMEM((rows, width), f32),
            pltpu.VMEM((rows, width), f32),
            pltpu.VMEM((rows, width), f32),
            pltpu.VMEM((rows, width), f32),
            pltpu.VMEM((keys, 3 * D), jnp.bfloat16),
            pltpu.VMEM((keys, 3 * D), jnp.bfloat16),
            pltpu.VMEM((2 * D, keys), jnp.bfloat16),
            pltpu.VMEM((2 * D, keys), jnp.bfloat16),
            dma((2, heads)),
            dma((2, total_steps)),
            dma((heads, devices - 1)),
            dma((heads, devices - 1)),
            dma((heads, nz - 1)),
            dma((heads, nz - 1)),
            dma((heads, nz)),
            dma((heads, nz)),
            dma((heads, 2)),
            dma((heads, 2)),
            dma((heads,)),
            dma((heads,)),
            dma((heads, nz)),
            dma((heads, nz)),
            dma((heads, nz - 1)),
            dma((heads, nz - 1)),
            dma((heads, devices - 1)),
            dma((heads, devices - 1)),
        ],
        compiler_params=pltpu.CompilerParams(
            collective_id=0, has_side_effects=True, vmem_limit_bytes=60 * 1024 * 1024
        ),
    )(k, v, gate[None, :], lists, place[None, :], q, g)


def local(
    queries,
    visual_keys,
    visual_value_rows,
    output_gradient,
    query_head_gate,
    window_lists,
    block_place,
):
    row_count = queries.shape[0]
    feature_width = visual_keys.shape[1]
    list_len = window_lists.shape[1]
    devices = lax.axis_size("seq")
    window_devices = WINDOW_ROWS // row_count
    blocks_here = visual_keys.shape[0] // BLOCK_TOKENS
    piece_len = BLOCK_TOKENS // devices
    channels = 2 * feature_width
    positions = devices * blocks_here
    one_window = window_lists.shape[0] == 1 and devices == window_devices and blocks_here == 1
    if one_window and devices % 4 == 0 and devices > 4 and feature_width == 4 * D:
        return fused(
            queries,
            output_gradient,
            visual_keys,
            visual_value_rows,
            query_head_gate,
            window_lists,
            block_place,
        )
    stacked = jnp.concatenate([visual_keys, visual_value_rows], axis=1)
    stacked = stacked.reshape(blocks_here, devices, piece_len, channels)
    spread = lax.all_to_all(stacked, "seq", split_axis=1, concat_axis=0, tiled=True).reshape(
        positions, piece_len, channels
    )
    target_window = jnp.arange(devices, dtype=jnp.int32) // window_devices
    wanted = jnp.take(block_place, jnp.take(window_lists, target_window, axis=0), axis=0)
    fetched = lax.all_to_all(spread[wanted], "seq", split_axis=0, concat_axis=2, tiled=True)
    fetched = fetched.reshape(list_len * BLOCK_TOKENS, channels)
    output, grad_query, grad_key, grad_value = attend(
        queries,
        output_gradient,
        gate_row_of(query_head_gate),
        fetched[:, :feature_width],
        fetched[:, feature_width:],
    )
    gradients = jnp.concatenate([grad_key, grad_value], axis=1)
    collected = lax.all_to_all(
        gradients.reshape(list_len, devices, piece_len, channels),
        "seq",
        split_axis=1,
        concat_axis=1,
        tiled=True,
    )
    onehot = (wanted.T.reshape(1, -1) == jnp.arange(positions, dtype=jnp.int32)[:, None]).astype(
        jnp.float32
    )
    summed = jnp.dot(
        onehot,
        collected.reshape(list_len * devices, piece_len * channels),
        precision=HIGHEST,
        preferred_element_type=jnp.float32,
    )
    returned = lax.all_to_all(
        summed.reshape(devices, blocks_here, piece_len, channels),
        "seq",
        split_axis=0,
        concat_axis=2,
        tiled=True,
    )
    returned = returned.reshape(blocks_here * BLOCK_TOKENS, channels)
    return (output, grad_query, returned[:, :feature_width], returned[:, feature_width:])


def solution(mesh):
    rows = P(("parts", "seq"), None)
    return jax.shard_map(
        local,
        mesh=mesh,
        in_specs=(rows, rows, rows, rows, P(), P("parts", None), P("parts")),
        out_specs=(rows, rows, rows, rows),
        check_vma=False,
    )
```
